32 devices in a mesh: groups: 2 (over y), ctx: 4 (over z), head: 2 (over x), sess: 2 (over core).
Axes of the slice: x: 2, y: 2, z: 4, core: 2. Of those that a mesh axis runs over, the one named last changes fastest.
Arguments:
- head_input: bfloat16 [8, 512, 8192], P(('groups', 'sess'), 'ctx', 'head'), parts along dimension 0, may hold values from -6 to 6
- gate_input: bfloat16 [8, 512, 8192], P(('groups', 'sess'), 'ctx', 'head'), parts along dimension 0, may hold values from -6 to 6
- state_in_proj: bfloat16 [8, 512, 8, 128], P(('groups', 'sess'), 'ctx'), parts along dimension 0, may hold values from -1.796875 to 1.796875
- state_out_proj: bfloat16 [8, 512, 8, 128], P(('groups', 'sess'), 'ctx'), parts along dimension 0, may hold values from -1.796875 to 1.796875
- step_raw: float32 [8, 512, 128], P(('groups', 'sess'), 'ctx', 'head'), parts along dimension 0, may hold values from -2.5 to 12.5
- head_step_bias: float32 [128], P('head'), may hold values from -5.3 to -2.25
- decay_log: float32 [128], P('head'), may hold values from -7.7 to 0
- skip_gain: float32 [128], P('head'), may hold values from 0.5 to 2
- norm_gain: float32 [8192], P('head'), may hold values from 0.1 to 1.9
- out_weight: bfloat16 [8192, 4096], P('head', 'ctx'), may hold values from -0.09375 to 0.09375
- pool_states: float32 [16, 128, 64, 128], P(('groups', 'sess'), 'head', None, 'ctx'), parts along dimension 0, may hold values from -6 to 6
- slot_map: int32 [8], P('groups'), parts along dimension 0, may hold values from 0 to 7, as said below
- span_lengths: int32 [8], P('groups'), parts along dimension 0, may hold values from 1 to 4, as said below
Outputs:
- mixed: bfloat16 [8, 512, 4096], P(('groups', 'sess'), 'ctx', 'head'), parts along dimension 0
- final_states: float32 [8, 128, 64, 128], P(('groups', 'sess'), 'head', None, 'ctx'), parts along dimension 0
The draws below stay inside these ranges and needn't reach their ends.
There are 2 independent parts, one for each index of `groups`. The reference program is written for one: setup_inputs(seed, part) draws one part's arguments, and reference() takes and returns one part's arrays. A program takes and returns all parts, laid end to end along the dimension named above; an argument that names none is the same for every part. Nothing has to cross between parts.
Inputs may be any that keep to these rules, and one draw needn't show every extreme that they name: `slot_map`: the sessions of a group take distinct decode slots. `span_lengths`: some session of every group fills all 4 units.
All inputs are finite; a program needn't handle non-finite values.
Results may differ from the reference program's by a relative error of at most 0.018.
Values may be sent and summed in bfloat16 or wider, within the bound.
A program may use at most 128 MiB of HBM per device.

```python
import math
import jax
import jax.numpy as jnp
from jax import lax

D_WIN = 4096
HEADS = 128
HEAD_DIM = 64
STATE = 128
GROUPS = 8
SPAN = 128
SESS_DEV = 2
RESULT_LENGTH = 512
SPANS = 4
GROUP_SESSIONS = 4
SLOTS = 8
N_HEAD = 2


def draw_step_raw(key, part):
    base_key = jax.random.fold_in(key, 11)
    flurry_random_key = jax.random.fold_in(key, 12)
    starting_values = jnp.clip(0.5 * jax.random.normal(base_key, (GROUP_SESSIONS, RESULT_LENGTH, HEADS), jnp.float32), -2.5, 2.5)
    flurry_lengths = (jax.random.randint(flurry_random_key, (GROUP_SESSIONS, RESULT_LENGTH, 1), 0, 1024) == 0).astype(jnp.float32)
    return starting_values + 10.0 * flurry_lengths


def draw_decay_log(key, part):
    rate_key = jax.random.fold_in(key, 21)
    return jax.random.uniform(rate_key, (HEADS,), jnp.float32, math.log(0.001), 0.0)


def draw_slot_map(key, part):
    middle = (jax.random.permutation(jax.random.fold_in(key, 31), SLOTS - 2)[:GROUP_SESSIONS - 2] + 1).astype(jnp.int32)
    high_session = jax.random.randint(jax.random.fold_in(key, 33), (), 0, SESS_DEV)
    low_session = GROUP_SESSIONS - SESS_DEV + jax.random.randint(jax.random.fold_in(key, 34), (), 0, SESS_DEV)
    index_values = jnp.arange(GROUP_SESSIONS, dtype=jnp.int32)
    special = (index_values == high_session) | (index_values == low_session)
    others_rank = jnp.cumsum(jnp.where(special, 0, 1)) - 1
    others_rank = jnp.clip(others_rank, 0, GROUP_SESSIONS - 3).astype(jnp.int32)
    filled = middle[others_rank]
    result = jnp.where(index_values == high_session, SLOTS - 1, jnp.where(index_values == low_session, 0, filled))
    return result.astype(jnp.int32)


def draw_span_lengths(key, part):
    base_len = jax.random.randint(jax.random.fold_in(key, 41), (GROUP_SESSIONS,), 1, SPANS + 1)
    full_one = jax.random.randint(jax.random.fold_in(key, 42), (), 0, GROUP_SESSIONS)
    return jnp.where(jnp.arange(GROUP_SESSIONS) == full_one, SPANS, base_len).astype(jnp.int32)


def strengthened(values, stream_key, source, target, shards_of, factor):
    def block_of(dim):
        return (jnp.arange(values.shape[dim]) // (values.shape[dim] // shards_of)).reshape((-1,) + (1,) * (values.ndim - 1 - dim))

    first = jax.random.permutation(stream_key, shards_of)[block_of(target)]
    far = (block_of(target) + shards_of // 2) % shards_of
    return jnp.where((block_of(source) == first) | (block_of(source) == far), factor * values, values)


def shard_levels(key, dims, pieces, least, high):
    def one(axis_at, blocks):
        draws = jax.random.uniform(jax.random.fold_in(jax.random.fold_in(key, 6), axis_at), (blocks,), jnp.float32, least / len(pieces), high / len(pieces))
        return jnp.repeat(jnp.exp(draws), dims[axis_at] // blocks).reshape((-1,) + (1,) * (len(dims) - axis_at - 1))

    gain = one(*pieces[0])
    for cut in pieces[1:]:
        gain = gain * one(*cut)
    return gain


def bell_draw(stream_key, extent, scale, limit, cuts=(), held_as=jnp.bfloat16):
    array = scale * jax.random.normal(stream_key, extent, jnp.float32)
    if cuts:
        array = array * shard_levels(stream_key, extent, cuts, -0.22, 0.18)
    return jnp.clip(array, -limit, limit).astype(held_as)


def gaussian_with(own_key, shape, deviation, reach, shards, heavy, kind=jnp.bfloat16):
    values = deviation * jax.random.normal(own_key, shape, jnp.float32)
    if shards:
        values = values * shard_levels(own_key, shape, shards, -0.22, 0.18)
    return jnp.clip(strengthened(values, jax.random.fold_in(own_key, 3), *heavy), -reach, reach).astype(kind)


def setup_inputs(seed: int = 0, part: int = 0) -> dict:
    splits = jax.random.split(jax.random.key(seed), 14)
    part_splits = jax.random.split(jax.random.fold_in(splits[13], part), 14)
    return {
        "head_input": bell_draw(part_splits[0], (GROUP_SESSIONS, RESULT_LENGTH, HEADS * HEAD_DIM), 1.0, 6.0, ((0, 2), (1, 4), (2, 2))),
        "gate_input": bell_draw(part_splits[1], (GROUP_SESSIONS, RESULT_LENGTH, HEADS * HEAD_DIM), 1.0, 6.0, ((0, 2), (1, 4), (2, 2))),
        "state_in_proj": bell_draw(part_splits[2], (GROUP_SESSIONS, RESULT_LENGTH, GROUPS, STATE), 0.3, 1.796875, ((0, 2), (1, 4))),
        "state_out_proj": bell_draw(part_splits[3], (GROUP_SESSIONS, RESULT_LENGTH, GROUPS, STATE), 0.3, 1.796875, ((0, 2), (1, 4))),
        "step_raw": draw_step_raw(jax.random.fold_in(jax.random.fold_in(splits[13], part), 71), part),
        "head_step_bias": jnp.clip(-5.3 + 3.0500002 * jax.random.uniform(splits[5], (HEADS,), jnp.float32) ** shard_levels(splits[5], (HEADS,), ((0, 2),), -0.2, 0.2), -5.3, -2.25),
        "decay_log": draw_decay_log(jax.random.fold_in(splits[13], 71), part),
        "skip_gain": jnp.clip(0.5 + 1.5 * jax.random.uniform(splits[7], (HEADS,), jnp.float32) ** shard_levels(splits[7], (HEADS,), ((0, 2),), -0.2, 0.2), 0.5, 2.0),
        "norm_gain": jnp.clip(1.0 + 0.18 * jax.random.normal(splits[8], (HEADS * HEAD_DIM,), jnp.float32), 0.1, 1.9),
        "out_weight": gaussian_with(splits[9], (HEADS * HEAD_DIM, D_WIN), (HEADS * HEAD_DIM) ** -0.5, 0.09375, ((0, 2), (1, 4)), (0, 1, 4, 2.0)),
        "pool_states": bell_draw(part_splits[10], (SLOTS, HEADS, HEAD_DIM, STATE), 1.0, 6.0, ((0, 2), (1, 2), (3, 4)), jnp.float32),
        "slot_map": draw_slot_map(jax.random.fold_in(jax.random.fold_in(splits[13], part), 71), part),
        "span_lengths": draw_span_lengths(jax.random.fold_in(jax.random.fold_in(splits[13], part), 71), part),
    }


def reference(head_input, gate_input, state_in_proj, state_out_proj, step_raw, head_step_bias, decay_log, skip_gain, norm_gain, out_weight, pool_states, slot_map, span_lengths):
    group_heads = HEADS // GROUPS
    position = jnp.arange(RESULT_LENGTH, dtype=jnp.int32)
    decay_rate = jnp.exp(decay_log)
    block_rows = HEADS * HEAD_DIM // N_HEAD
    mixed_rows = []
    final_rows = []
    for session in range(GROUP_SESSIONS):
        live_rows = (position < span_lengths[session] * SPAN).astype(jnp.float32)
        step_size = jax.nn.softplus(step_raw[session] + head_step_bias[None, :]) * live_rows[:, None]
        keep_rows = jnp.exp(-decay_rate[None, :] * step_size)
        inputs = head_input[session].astype(jnp.float32).reshape(RESULT_LENGTH, HEADS, HEAD_DIM)

        def advance(carried, stepped):
            x_token, b_token, c_token, size_token, keep_token = stepped
            b_heads = jnp.repeat(b_token.astype(jnp.float32), group_heads, axis=0)
            c_heads = jnp.repeat(c_token.astype(jnp.float32), group_heads, axis=0)
            carried = keep_token[:, None, None] * carried + (size_token[:, None] * x_token)[:, :, None] * b_heads[:, None, :]
            return (carried, lax.optimization_barrier(jnp.sum(carried * c_heads[:, None, :], axis=2)))
        start_state = pool_states[slot_map[session]]
        final_state, outputs = lax.scan(advance, start_state, (inputs, state_in_proj[session], state_out_proj[session], step_size, keep_rows))
        ssd_out = outputs + skip_gain[None, :, None] * inputs
        gated = ssd_out.reshape(RESULT_LENGTH, HEADS * HEAD_DIM) * jax.nn.silu(gate_input[session].astype(jnp.float32))
        grouped = gated.reshape(RESULT_LENGTH, GROUPS, group_heads * HEAD_DIM)
        norm_scale = lax.rsqrt(lax.optimization_barrier(jnp.mean(grouped * grouped, axis=2, keepdims=True)) + 1e-05)
        normed = ((grouped * norm_scale).reshape(RESULT_LENGTH, HEADS * HEAD_DIM) * norm_gain).astype(jnp.bfloat16)
        summed = jnp.zeros((RESULT_LENGTH, D_WIN), jnp.float32)
        for block_index in range(N_HEAD):
            low = block_index * block_rows
            partial_term = jnp.dot(normed[:, low:low + block_rows], out_weight[low:low + block_rows], preferred_element_type=jnp.float32)
            partial_term = lax.optimization_barrier(partial_term.astype(jnp.bfloat16))
            summed = summed + partial_term.astype(jnp.float32)
        mixed_rows.append((summed * live_rows[:, None]).astype(jnp.bfloat16))
        final_rows.append(final_state)
    return (jnp.stack(mixed_rows), jnp.stack(final_rows))
```

```python
import functools

import jax
import jax.numpy as jnp
from jax import lax
from jax.experimental import pallas as pl
from jax.experimental.pallas import tpu as pltpu
from jax.sharding import PartitionSpec as P

HEADS = 128
GROUPS = 8
SPAN = 128
CHUNKS = 4
VMEM_LIMIT = 40 * 1024 * 1024

norm_eps = 1e-05
f32 = jnp.float32
bf16 = jnp.bfloat16


def swapped(value, axis):
    length = lax.axis_size(axis)
    return lax.ppermute(value, axis, [(i, length - 1 - i) for i in range(length)])


def spread(values, head_dim):
    heads = values.shape[1]
    rows = lax.broadcasted_iota(jnp.int32, (heads, heads * head_dim), 0)
    cols = lax.broadcasted_iota(jnp.int32, (heads, heads * head_dim), 1)
    inside = (cols >= rows * head_dim) & (cols < (rows + 1) * head_dim)
    return jnp.dot(
        values,
        inside.astype(f32),
        precision=lax.Precision.HIGHEST,
        preferred_element_type=f32,
    )


def local_end_kernel(head_dim, x_ref, b_ref, w_ref, o_ref):
    weighted = (x_ref[0].astype(f32) * spread(w_ref[0, 0], head_dim)).astype(bf16)
    state = lax.dot_general(
        b_ref[0, 0], weighted, (((0,), (0,)), ((), ())), preferred_element_type=f32
    )
    owners, _, cols, channels = o_ref.shape
    o_ref[:, 0] = state.reshape(owners, cols, channels).astype(bf16)


def normed_kernel(
    head_dim,
    x_ref,
    z_ref,
    b_ref,
    c_ref,
    cum_ref,
    cum_t_ref,
    size_t_ref,
    carry_ref,
    skip_ref,
    gain_ref,
    o_ref,
    y_ref,
):
    tokens, channels = x_ref.shape[1:]
    heads = cum_ref.shape[3]
    c_mat = c_ref[0, 0]
    products = lax.dot_general(
        c_mat, b_ref[0, 0], (((1,), (1,)), ((), ())), preferred_element_type=f32
    )
    rows = lax.broadcasted_iota(jnp.int32, (tokens, tokens), 0)
    cols = lax.broadcasted_iota(jnp.int32, (tokens, tokens), 1)
    causal = rows >= cols
    cum = cum_ref[0, 0]
    cum_t = cum_t_ref[0, 0]
    size_t = size_t_ref[0, 0]
    width = 2 * head_dim
    first = lax.broadcasted_iota(jnp.int32, (tokens, width), 1) < head_dim

    def scores(h):
        gap = cum[:, h : h + 1] - cum_t[h : h + 1, :]
        decay = jnp.exp(jnp.where(causal, gap, -1e30))
        return (products * decay * size_t[h : h + 1, :]).astype(bf16)

    for pair in range(heads // 2):
        both = jnp.concatenate([scores(2 * pair), scores(2 * pair + 1)], axis=1)
        x_pair = x_ref[0, :, pair * width : (pair + 1) * width]
        none = jnp.zeros_like(x_pair)
        split = jnp.concatenate(
            [jnp.where(first, x_pair, none), jnp.where(first, none, x_pair)], axis=0
        )
        y_ref[:, pair * width : (pair + 1) * width] = jnp.dot(
            both, split, preferred_element_type=f32
        )
    carry = carry_ref[:, 0].astype(f32).reshape(-1, channels).astype(bf16)
    carried = jnp.dot(c_mat, carry, preferred_element_type=f32)
    carried = carried * spread(jnp.exp(cum), head_dim)
    y = y_ref[...] + carried + skip_ref[...] * x_ref[0].astype(f32)
    z = z_ref[0].astype(f32)
    gated = y * (z / (1.0 + jnp.exp(-z)))
    scale = lax.rsqrt(jnp.mean(gated * gated, axis=1, keepdims=True) + norm_eps)
    o_ref[0] = (gated * scale * gain_ref[...]).astype(bf16)


def project_kernel(order_ref, a_ref, *refs):
    weights, o_ref = refs[:-1], refs[-1]
    depth = weights[0].shape[1]
    total = jnp.zeros(o_ref.shape[1:], f32)
    for i, w_ref in enumerate(weights):
        start = pl.multiple_of(order_ref[i] * depth, depth)
        total = total + jnp.dot(
            a_ref[:, pl.ds(start, depth)], w_ref[0], preferred_element_type=f32
        )
    o_ref[0] = total.astype(bf16)


def params(**more):
    return pltpu.CompilerParams(vmem_limit_bytes=VMEM_LIMIT, **more)


def shards(
    head_input,
    gate_input,
    state_in_proj,
    state_out_proj,
    step_raw,
    head_step_bias,
    decay_log,
    skip_gain,
    norm_gain,
    out_weight,
    pool_states,
    slot_map,
    span_lengths,
):
    ctx_count = lax.axis_size("ctx")
    ctx_index = lax.axis_index("ctx")
    sess_index = lax.axis_index("sess")
    head_index = lax.axis_index("head")
    group_index = lax.axis_index("groups")
    group_axis = lax.axis_size("groups")
    sess_axis = lax.axis_size("sess")
    sessions, tokens, inner = head_input.shape
    heads = step_raw.shape[2]
    head_dim = inner // heads
    state_cols = pool_states.shape[3]
    state_size = state_in_proj.shape[3]
    group_heads = HEADS // GROUPS
    count = heads // group_heads
    channels = group_heads * head_dim
    first_session = sess_index * sessions

    replicas = group_axis * sess_axis
    depth = out_weight.shape[0] // replicas
    own_cols = out_weight.shape[1]
    chunk_cols = own_cols // CHUNKS
    quarter = lax.dynamic_slice_in_dim(
        out_weight, (group_index * sess_axis + sess_index) * depth, depth, 0
    )
    weights = []
    for k in range(CHUNKS):
        mine = lax.all_gather(quarter[:, k * chunk_cols : (k + 1) * chunk_cols], "ctx", axis=0)
        across = swapped(mine, "groups")
        weights.append((mine, swapped(mine, "sess"), across, swapped(across, "sess")))
    other_group = group_axis - 1 - group_index
    other_sess = sess_axis - 1 - sess_index
    order = jnp.stack(
        [
            group_index * sess_axis + sess_index,
            group_index * sess_axis + other_sess,
            other_group * sess_axis + sess_index,
            other_group * sess_axis + other_sess,
        ]
    ).astype(jnp.int32)

    pooled = lax.all_gather(pool_states.astype(bf16), "sess", axis=0, tiled=True)
    own_slots = lax.dynamic_slice_in_dim(slot_map, first_session, sessions)
    start = jnp.take(pooled, own_slots, axis=0).astype(f32)
    start = jnp.transpose(start, (0, 3, 1, 2)).reshape(sessions, state_cols, inner)

    own_lengths = lax.dynamic_slice_in_dim(span_lengths, first_session, sessions)
    position = ctx_index * tokens + jnp.arange(tokens, dtype=jnp.int32)
    live_rows = (position[None, :] < own_lengths[:, None] * SPAN).astype(f32)
    size = jax.nn.softplus(step_raw + head_step_bias) * live_rows[:, :, None]
    log_keep = -jnp.exp(decay_log) * size
    lower = jnp.tril(jnp.ones((tokens, tokens), f32))
    cum = jnp.einsum("lm,smh->slh", lower, log_keep, precision=lax.Precision.HIGHEST)
    shard_log = cum[:, -1, :]
    tail = jnp.exp(cum[:, -1:, :] - cum) * size

    def by_group(value):
        return jnp.moveaxis(value.reshape(sessions, tokens, count, group_heads), 2, 1)

    def by_group_t(value):
        return jnp.transpose(value, (0, 2, 1)).reshape(sessions, count, group_heads, tokens)

    first_group = head_index * heads // group_heads
    b_groups = jnp.moveaxis(lax.dynamic_slice_in_dim(state_in_proj, first_group, count, 2), 2, 1)
    c_groups = jnp.moveaxis(lax.dynamic_slice_in_dim(state_out_proj, first_group, count, 2), 2, 1)

    wide = pl.BlockSpec((1, tokens, channels), lambda s, g: (s, 0, g))
    square = pl.BlockSpec((1, 1, tokens, state_size), lambda s, g: (s, g, 0, 0))
    tall = pl.BlockSpec((1, 1, tokens, group_heads), lambda s, g: (s, g, 0, 0))
    flat = pl.BlockSpec((1, 1, group_heads, tokens), lambda s, g: (s, g, 0, 0))
    states = pl.BlockSpec((ctx_count, 1, state_cols, channels), lambda s, g: (0, s, 0, g))
    line = pl.BlockSpec((1, channels), lambda s, g: (0, g))
    work = sessions * count * tokens

    local_end = pl.pallas_call(
        functools.partial(local_end_kernel, head_dim),
        grid=(sessions, count),
        in_specs=[wide, square, tall],
        out_specs=states,
        out_shape=jax.ShapeDtypeStruct((ctx_count, sessions, state_cols, inner), bf16),
        compiler_params=params(),
        cost_estimate=pl.CostEstimate(
            flops=2 * work * state_size * channels,
            bytes_accessed=4 * work * channels,
            transcendentals=0,
        ),
    )(head_input, b_groups, by_group(tail))

    ends = lax.all_to_all(local_end, "ctx", 0, 0)
    logs = lax.all_to_all(
        jnp.broadcast_to(shard_log, (ctx_count,) + shard_log.shape), "ctx", 0, 0
    )
    decays = jnp.repeat(jnp.exp(logs), head_dim, axis=2)
    running = start
    entering = []
    for j in range(ctx_count):
        entering.append(running.astype(bf16))
        running = decays[j][:, None, :] * running + ends[j].astype(f32)
    final_states = jnp.transpose(
        running.reshape(sessions, state_cols, heads, head_dim), (0, 2, 3, 1)
    )
    carried = lax.all_to_all(jnp.stack(entering), "ctx", 0, 0)

    normed = pl.pallas_call(
        functools.partial(normed_kernel, head_dim),
        grid=(sessions, count),
        in_specs=[wide, wide, square, square, tall, flat, flat, states, line, line],
        out_specs=wide,
        out_shape=jax.ShapeDtypeStruct((sessions, tokens, inner), bf16),
        scratch_shapes=[pltpu.VMEM((tokens, channels), f32)],
        compiler_params=params(),
        cost_estimate=pl.CostEstimate(
            flops=2 * work * channels * 3 * state_size,
            bytes_accessed=8 * work * channels,
            transcendentals=work * (channels + tokens * group_heads),
        ),
    )(
        head_input,
        gate_input,
        b_groups,
        c_groups,
        by_group(cum),
        by_group_t(cum),
        by_group_t(size),
        carried,
        jnp.repeat(skip_gain, head_dim)[None, :],
        norm_gain[None, :],
    ).reshape(sessions * tokens, inner)

    rows = sessions * tokens
    parts = []
    for chunk in weights:
        parts.append(
            pl.pallas_call(
                project_kernel,
                grid_spec=pltpu.PrefetchScalarGridSpec(
                    num_scalar_prefetch=1,
                    grid=(ctx_count,),
                    in_specs=[pl.BlockSpec((rows, inner), lambda c, order: (0, 0))]
                    + [pl.BlockSpec((1, depth, chunk_cols), lambda c, order: (c, 0, 0))] * replicas,
                    out_specs=pl.BlockSpec((1, rows, chunk_cols), lambda c, order: (c, 0, 0)),
                ),
                out_shape=jax.ShapeDtypeStruct((ctx_count, rows, chunk_cols), bf16),
                compiler_params=params(),
                cost_estimate=pl.CostEstimate(
                    flops=2 * rows * inner * ctx_count * chunk_cols,
                    bytes_accessed=2 * inner * (rows + ctx_count * chunk_cols),
                    transcendentals=0,
                ),
            )(order, normed, *chunk)
        )
    own_shards = ctx_count // lax.axis_size("head")
    if own_shards * 2 == ctx_count:
        sums = []
        for part in parts:
            kept = lax.dynamic_slice_in_dim(part, head_index * own_shards, own_shards)
            sent = lax.dynamic_slice_in_dim(part, (1 - head_index) * own_shards, own_shards)
            sums.append(kept.astype(f32) + swapped(sent, "head").astype(f32))
        summed = jnp.stack(sums, axis=1)
    else:
        summed = lax.psum_scatter(
            jnp.stack(parts, axis=1), "head", scatter_dimension=0, tiled=True
        ).astype(f32)
    summed = summed.reshape(own_shards, CHUNKS, sessions, tokens, chunk_cols)
    summed = jnp.transpose(summed, (2, 3, 0, 1, 4)).reshape(sessions, tokens, -1)
    mixed = (summed * live_rows[:, :, None]).astype(bf16)
    return (mixed, final_states)


def solution(mesh):
    placed = (
        P(("groups", "sess"), "ctx", "head"),
        P(("groups", "sess"), "ctx", "head"),
        P(("groups", "sess"), "ctx", None, None),
        P(("groups", "sess"), "ctx", None, None),
        P(("groups", "sess"), "ctx", "head"),
        P("head"),
        P("head"),
        P("head"),
        P("head"),
        P("head", "ctx"),
        P(("groups", "sess"), "head", None, "ctx"),
        P("groups"),
        P("groups"),
    )
    return jax.shard_map(
        shards,
        mesh=mesh,
        in_specs=placed,
        out_specs=(
            P(("groups", "sess"), "ctx", "head"),
            P(("groups", "sess"), "head", None, "ctx"),
        ),
        check_vma=False,
    )
```

```python
import functools

import jax
import jax.numpy as jnp
from jax import lax
from jax.experimental import pallas as pl
from jax.experimental.pallas import tpu as pltpu
from jax.sharding import PartitionSpec as P

HEADS = 128
GROUPS = 8
SPAN = 128
CHUNK_EIGHTHS = (2, 2, 2, 1, 1)
TIED = ((2, 3), (3, 5))
VMEM_LIMIT = 40 * 1024 * 1024

norm_eps = 1e-05
f32 = jnp.float32
bf16 = jnp.bfloat16


def swapped(value, axis):
    length = lax.axis_size(axis)
    return lax.ppermute(value, axis, [(i, length - 1 - i) for i in range(length)])


def spread(values, head_dim):
    heads = values.shape[1]
    rows = lax.broadcasted_iota(jnp.int32, (heads, heads * head_dim), 0)
    cols = lax.broadcasted_iota(jnp.int32, (heads, heads * head_dim), 1)
    inside = (cols >= rows * head_dim) & (cols < (rows + 1) * head_dim)
    return jnp.dot(
        values,
        inside.astype(f32),
        precision=lax.Precision.HIGHEST,
        preferred_element_type=f32,
    )


def local_end_kernel(head_dim, x_ref, b_ref, w_ref, o_ref):
    weighted = (x_ref[0].astype(f32) * spread(w_ref[0, 0], head_dim)).astype(bf16)
    state = lax.dot_general(
        b_ref[0, 0], weighted, (((0,), (0,)), ((), ())), preferred_element_type=f32
    )
    owners, _, cols, channels = o_ref.shape
    o_ref[:, 0] = state.reshape(owners, cols, channels).astype(bf16)


def combine_kernel(
    head_dim, slots_ref, ends_ref, logs_ref, own_ref, other_ref, enter_ref, final_ref
):
    heads = own_ref.shape[1]
    decays = spread(jnp.exp(logs_ref[0, 0]), head_dim)
    own = jnp.concatenate([own_ref[0, h] for h in range(heads)], axis=1)
    other = jnp.concatenate([other_ref[0, h].astype(f32) for h in range(heads)], axis=1)
    running = jnp.where(slots_ref[1, pl.program_id(0)] == 0, own, other)
    for j in range(ends_ref.shape[0]):
        enter_ref[j, 0] = running.astype(bf16)
        running = decays[j : j + 1, :] * running + ends_ref[j, 0].astype(f32)
    for h in range(heads):
        final_ref[0, h] = running[:, h * head_dim : (h + 1) * head_dim]


def normed_kernel(
    head_dim,
    x_ref,
    z_ref,
    b_ref,
    c_ref,
    cum_ref,
    cum_t_ref,
    size_t_ref,
    carry_ref,
    skip_ref,
    gain_ref,
    o_ref,
    y_ref,
):
    tokens, channels = x_ref.shape[1:]
    heads = cum_ref.shape[3]
    c_mat = c_ref[0, 0]
    products = lax.dot_general(
        c_mat, b_ref[0, 0], (((1,), (1,)), ((), ())), preferred_element_type=f32
    )
    rows = lax.broadcasted_iota(jnp.int32, (tokens, tokens), 0)
    cols = lax.broadcasted_iota(jnp.int32, (tokens, tokens), 1)
    causal = rows >= cols
    cum = cum_ref[0, 0]
    cum_t = cum_t_ref[0, 0]
    size_t = size_t_ref[0, 0]
    width = 2 * head_dim
    first = lax.broadcasted_iota(jnp.int32, (tokens, width), 1) < head_dim

    def scores(h):
        gap = cum[:, h : h + 1] - cum_t[h : h + 1, :]
        decay = jnp.exp(jnp.where(causal, gap, -1e30))
        return (products * decay * size_t[h : h + 1, :]).astype(bf16)

    for pair in range(heads // 2):
        both = jnp.concatenate([scores(2 * pair), scores(2 * pair + 1)], axis=1)
        x_pair = x_ref[0, :, pair * width : (pair + 1) * width]
        none = jnp.zeros_like(x_pair)
        split = jnp.concatenate(
            [jnp.where(first, x_pair, none), jnp.where(first, none, x_pair)], axis=0
        )
        y_ref[:, pair * width : (pair + 1) * width] = jnp.dot(
            both, split, preferred_element_type=f32
        )
    carry = carry_ref[:, 0].astype(f32).reshape(-1, channels).astype(bf16)
    carried = jnp.dot(c_mat, carry, preferred_element_type=f32)
    carried = carried * spread(jnp.exp(cum), head_dim)
    y = y_ref[...] + carried + skip_ref[...] * x_ref[0].astype(f32)
    z = z_ref[0].astype(f32)
    gated = y * (z / (1.0 + jnp.exp(-z)))
    scale = lax.rsqrt(jnp.mean(gated * gated, axis=1, keepdims=True) + norm_eps)
    o_ref[0] = (gated * scale * gain_ref[...]).astype(bf16)


def project_kernel(order_ref, a_ref, *refs):
    weights, o_ref = refs[:-1], refs[-1]
    depth = weights[0].shape[1]
    total = jnp.zeros(o_ref.shape[1:], f32)
    for i, w_ref in enumerate(weights):
        start = pl.multiple_of(order_ref[i] * depth, depth)
        total = total + jnp.dot(
            a_ref[:, pl.ds(start, depth)], w_ref[0], preferred_element_type=f32
        )
    o_ref[0] = total.astype(bf16)


def params(**more):
    return pltpu.CompilerParams(vmem_limit_bytes=VMEM_LIMIT, **more)


def shards(
    head_input,
    gate_input,
    state_in_proj,
    state_out_proj,
    step_raw,
    head_step_bias,
    decay_log,
    skip_gain,
    norm_gain,
    out_weight,
    pool_states,
    slot_map,
    span_lengths,
):
    ctx_count = lax.axis_size("ctx")
    ctx_index = lax.axis_index("ctx")
    sess_index = lax.axis_index("sess")
    head_index = lax.axis_index("head")
    group_index = lax.axis_index("groups")
    group_axis = lax.axis_size("groups")
    sess_axis = lax.axis_size("sess")
    sessions, tokens, inner = head_input.shape
    heads = step_raw.shape[2]
    head_dim = inner // heads
    state_cols = pool_states.shape[3]
    state_size = state_in_proj.shape[3]
    group_heads = HEADS // GROUPS
    count = heads // group_heads
    channels = group_heads * head_dim
    first_session = sess_index * sessions

    replicas = group_axis * sess_axis
    depth = out_weight.shape[0] // replicas
    own_cols = out_weight.shape[1]
    unit = own_cols // 8
    first_row = (group_index * sess_axis + sess_index) * depth

    def gathered(k, after=None):
        offset = sum(CHUNK_EIGHTHS[:k]) * unit
        width = CHUNK_EIGHTHS[k] * unit
        block = lax.dynamic_slice(out_weight, (first_row, offset), (depth, width))
        if after is not None:
            block, after = lax.optimization_barrier((block, after))
        mine = lax.all_gather(block, "ctx", axis=0)
        across = swapped(mine, "groups")
        return (mine, swapped(mine, "sess"), across, swapped(across, "sess")), after

    weights = [gathered(k)[0] for k in range(TIED[0][0])]
    other_group = group_axis - 1 - group_index
    other_sess = sess_axis - 1 - sess_index
    order = jnp.stack(
        [
            group_index * sess_axis + sess_index,
            group_index * sess_axis + other_sess,
            other_group * sess_axis + sess_index,
            other_group * sess_axis + other_sess,
        ]
    ).astype(jnp.int32)

    own_pool = jnp.transpose(pool_states, (0, 1, 3, 2))
    other_pool = swapped(own_pool.astype(bf16), "sess")
    own_slots = lax.dynamic_slice_in_dim(slot_map, first_session, sessions)
    slots = jnp.stack([own_slots % own_pool.shape[0], own_slots // own_pool.shape[0] - sess_index])

    own_lengths = lax.dynamic_slice_in_dim(span_lengths, first_session, sessions)
    position = ctx_index * tokens + jnp.arange(tokens, dtype=jnp.int32)
    live_rows = (position[None, :] < own_lengths[:, None] * SPAN).astype(f32)
    size = jax.nn.softplus(step_raw + head_step_bias) * live_rows[:, :, None]
    log_keep = -jnp.exp(decay_log) * size
    lower = jnp.tril(jnp.ones((tokens, tokens), f32))
    cum = jnp.einsum("lm,smh->slh", lower, log_keep, precision=lax.Precision.HIGHEST)
    shard_log = cum[:, -1, :]
    tail = jnp.exp(cum[:, -1:, :] - cum) * size

    def by_group(value):
        return jnp.moveaxis(value.reshape(sessions, tokens, count, group_heads), 2, 1)

    def by_group_t(value):
        return jnp.transpose(value, (0, 2, 1)).reshape(sessions, count, group_heads, tokens)

    first_group = head_index * heads // group_heads
    b_groups = jnp.moveaxis(lax.dynamic_slice_in_dim(state_in_proj, first_group, count, 2), 2, 1)
    c_groups = jnp.moveaxis(lax.dynamic_slice_in_dim(state_out_proj, first_group, count, 2), 2, 1)

    wide = pl.BlockSpec((1, tokens, channels), lambda s, g: (s, 0, g))
    square = pl.BlockSpec((1, 1, tokens, state_size), lambda s, g: (s, g, 0, 0))
    tall = pl.BlockSpec((1, 1, tokens, group_heads), lambda s, g: (s, g, 0, 0))
    flat = pl.BlockSpec((1, 1, group_heads, tokens), lambda s, g: (s, g, 0, 0))
    states = pl.BlockSpec((ctx_count, 1, state_cols, channels), lambda s, g: (0, s, 0, g))
    line = pl.BlockSpec((1, channels), lambda s, g: (0, g))
    work = sessions * count * tokens

    local_end = pl.pallas_call(
        functools.partial(local_end_kernel, head_dim),
        grid=(sessions, count),
        in_specs=[wide, square, tall],
        out_specs=states,
        out_shape=jax.ShapeDtypeStruct((ctx_count, sessions, state_cols, inner), bf16),
        compiler_params=params(),
        cost_estimate=pl.CostEstimate(
            flops=2 * work * state_size * channels,
            bytes_accessed=4 * work * channels,
            transcendentals=0,
        ),
    )(head_input, b_groups, by_group(tail))

    ends = lax.all_to_all(local_end, "ctx", 0, 0)
    logs = lax.all_to_all(
        jnp.broadcast_to(shard_log, (ctx_count,) + shard_log.shape), "ctx", 0, 0
    )
    logs = jnp.transpose(logs.reshape(ctx_count, sessions, count, group_heads), (1, 2, 0, 3))
    pool_block = pl.BlockSpec(
        (1, group_heads, state_cols, head_dim), lambda s, g, slots: (slots[0, s], g, 0, 0)
    )
    states_p = pl.BlockSpec(
        (ctx_count, 1, state_cols, channels), lambda s, g, slots: (0, s, 0, g)
    )
    entering, final = pl.pallas_call(
        functools.partial(combine_kernel, head_dim),
        grid_spec=pltpu.PrefetchScalarGridSpec(
            num_scalar_prefetch=1,
            grid=(sessions, count),
            in_specs=[
                states_p,
                pl.BlockSpec((1, 1, ctx_count, group_heads), lambda s, g, slots: (s, g, 0, 0)),
                pool_block,
                pool_block,
            ],
            out_specs=[
                states_p,
                pl.BlockSpec(
                    (1, group_heads, state_cols, head_dim), lambda s, g, slots: (s, g, 0, 0)
                ),
            ],
        ),
        out_shape=[
            jax.ShapeDtypeStruct((ctx_count, sessions, state_cols, inner), bf16),
            jax.ShapeDtypeStruct((sessions, heads, state_cols, head_dim), f32),
        ],
        compiler_params=params(),
        cost_estimate=pl.CostEstimate(
            flops=3 * ctx_count * sessions * state_cols * inner,
            bytes_accessed=6 * ctx_count * sessions * state_cols * inner,
            transcendentals=0,
        ),
    )(slots, ends, logs, own_pool, other_pool)
    final_states = jnp.transpose(final, (0, 1, 3, 2))
    for k in range(*TIED[0]):
        chunk, entering = gathered(k, entering)
        weights.append(chunk)
    carried = lax.all_to_all(entering, "ctx", 0, 0)

    normed = pl.pallas_call(
        functools.partial(normed_kernel, head_dim),
        grid=(sessions, count),
        in_specs=[wide, wide, square, square, tall, flat, flat, states, line, line],
        out_specs=wide,
        out_shape=jax.ShapeDtypeStruct((sessions, tokens, inner), bf16),
        scratch_shapes=[pltpu.VMEM((tokens, channels), f32)],
        compiler_params=params(),
        cost_estimate=pl.CostEstimate(
            flops=2 * work * channels * 3 * state_size,
            bytes_accessed=8 * work * channels,
            transcendentals=work * (channels + tokens * group_heads),
        ),
    )(
        head_input,
        gate_input,
        b_groups,
        c_groups,
        by_group(cum),
        by_group_t(cum),
        by_group_t(size),
        carried,
        jnp.repeat(skip_gain, head_dim)[None, :],
        norm_gain[None, :],
    ).reshape(sessions * tokens, inner)

    for k in range(*TIED[1]):
        chunk, normed = gathered(k, normed)
        weights.append(chunk)

    rows = sessions * tokens
    own_shards = ctx_count // lax.axis_size("head")
    sums = []
    for chunk in weights:
        chunk_cols = chunk[0].shape[2]
        part = pl.pallas_call(
            project_kernel,
            grid_spec=pltpu.PrefetchScalarGridSpec(
                num_scalar_prefetch=1,
                grid=(ctx_count,),
                in_specs=[pl.BlockSpec((rows, inner), lambda c, order: (0, 0))]
                + [pl.BlockSpec((1, depth, chunk_cols), lambda c, order: (c, 0, 0))] * replicas,
                out_specs=pl.BlockSpec((1, rows, chunk_cols), lambda c, order: (c, 0, 0)),
            ),
            out_shape=jax.ShapeDtypeStruct((ctx_count, rows, chunk_cols), bf16),
            compiler_params=params(),
            cost_estimate=pl.CostEstimate(
                flops=2 * rows * inner * ctx_count * chunk_cols,
                bytes_accessed=2 * inner * (rows + ctx_count * chunk_cols),
                transcendentals=0,
            ),
        )(order, normed, *chunk)
        if own_shards * 2 == ctx_count:
            kept = lax.dynamic_slice_in_dim(part, head_index * own_shards, own_shards)
            sent = lax.dynamic_slice_in_dim(part, (1 - head_index) * own_shards, own_shards)
            total = kept.astype(f32) + swapped(sent, "head").astype(f32)
        else:
            total = lax.psum_scatter(part, "head", scatter_dimension=0, tiled=True).astype(f32)
        total = total.reshape(own_shards, sessions, tokens, chunk_cols)
        sums.append((total * live_rows[None, :, :, None]).astype(bf16))
    mixed = jnp.concatenate(
        [total[shard] for shard in range(own_shards) for total in sums], axis=2
    )
    return (mixed, final_states)


def solution(mesh):
    placed = (
        P(("groups", "sess"), "ctx", "head"),
        P(("groups", "sess"), "ctx", "head"),
        P(("groups", "sess"), "ctx", None, None),
        P(("groups", "sess"), "ctx", None, None),
        P(("groups", "sess"), "ctx", "head"),
        P("head"),
        P("head"),
        P("head"),
        P("head"),
        P("head", "ctx"),
        P(("groups", "sess"), "head", None, "ctx"),
        P("groups"),
        P("groups"),
    )
    return jax.shard_map(
        shards,
        mesh=mesh,
        in_specs=placed,
        out_specs=(
            P(("groups", "sess"), "ctx", "head"),
            P(("groups", "sess"), "head", None, "ctx"),
        ),
        check_vma=False,
    )
```

```python
import functools

import jax
import jax.numpy as jnp
from jax import lax
from jax.experimental import pallas as pl
from jax.experimental.pallas import tpu as pltpu
from jax.sharding import PartitionSpec as P

HEADS = 128
GROUPS = 8
SPAN = 128
CHUNK_EIGHTHS = (2, 2, 2, 1, 1)
VMEM_LIMIT = 40 * 1024 * 1024

norm_eps = 1e-05
f32 = jnp.float32
bf16 = jnp.bfloat16


def swapped(value, axis):
    length = lax.axis_size(axis)
    return lax.ppermute(value, axis, [(i, length - 1 - i) for i in range(length)])


def spread(values, head_dim):
    heads = values.shape[1]
    rows = lax.broadcasted_iota(jnp.int32, (heads, heads * head_dim), 0)
    cols = lax.broadcasted_iota(jnp.int32, (heads, heads * head_dim), 1)
    inside = (cols >= rows * head_dim) & (cols < (rows + 1) * head_dim)
    return jnp.dot(
        values,
        inside.astype(f32),
        precision=lax.Precision.HIGHEST,
        preferred_element_type=f32,
    )


def local_end_kernel(head_dim, x_ref, b_ref, w_ref, o_ref):
    weighted = (x_ref[0].astype(f32) * spread(w_ref[0, 0], head_dim)).astype(bf16)
    state = lax.dot_general(
        b_ref[0, 0], weighted, (((0,), (0,)), ((), ())), preferred_element_type=f32
    )
    owners, _, cols, channels = o_ref.shape
    o_ref[:, 0] = state.reshape(owners, cols, channels).astype(bf16)


def combine_kernel(
    head_dim, slots_ref, ends_ref, logs_ref, own_ref, other_ref, enter_ref, final_ref
):
    heads = own_ref.shape[1]
    decays = spread(jnp.exp(logs_ref[0, 0]), head_dim)
    own = jnp.concatenate([own_ref[0, h] for h in range(heads)], axis=1)
    other = jnp.concatenate([other_ref[0, h].astype(f32) for h in range(heads)], axis=1)
    running = jnp.where(slots_ref[1, pl.program_id(0)] == 0, own, other)
    for j in range(ends_ref.shape[0]):
        enter_ref[j, 0] = running.astype(bf16)
        running = decays[j : j + 1, :] * running + ends_ref[j, 0].astype(f32)
    for h in range(heads):
        final_ref[0, h] = running[:, h * head_dim : (h + 1) * head_dim]


def normed_kernel(
    head_dim,
    x_ref,
    z_ref,
    b_ref,
    c_ref,
    cum_ref,
    cum_t_ref,
    size_t_ref,
    carry_ref,
    skip_ref,
    gain_ref,
    o_ref,
    y_ref,
):
    tokens, channels = x_ref.shape[1:]
    heads = cum_ref.shape[3]
    c_mat = c_ref[0, 0]
    products = lax.dot_general(
        c_mat, b_ref[0, 0], (((1,), (1,)), ((), ())), preferred_element_type=f32
    )
    rows = lax.broadcasted_iota(jnp.int32, (tokens, tokens), 0)
    cols = lax.broadcasted_iota(jnp.int32, (tokens, tokens), 1)
    causal = rows >= cols
    cum = cum_ref[0, 0]
    cum_t = cum_t_ref[0, 0]
    size_t = size_t_ref[0, 0]
    width = 2 * head_dim
    first = lax.broadcasted_iota(jnp.int32, (tokens, width), 1) < head_dim

    def scores(h):
        gap = cum[:, h : h + 1] - cum_t[h : h + 1, :]
        decay = jnp.exp(jnp.where(causal, gap, -1e30))
        return (products * decay * size_t[h : h + 1, :]).astype(bf16)

    for pair in range(heads // 2):
        both = jnp.concatenate([scores(2 * pair), scores(2 * pair + 1)], axis=1)
        x_pair = x_ref[0, :, pair * width : (pair + 1) * width]
        none = jnp.zeros_like(x_pair)
        split = jnp.concatenate(
            [jnp.where(first, x_pair, none), jnp.where(first, none, x_pair)], axis=0
        )
        y_ref[:, pair * width : (pair + 1) * width] = jnp.dot(
            both, split, preferred_element_type=f32
        )
    carry = carry_ref[:, 0].astype(f32).reshape(-1, channels).astype(bf16)
    carried = jnp.dot(c_mat, carry, preferred_element_type=f32)
    carried = carried * spread(jnp.exp(cum), head_dim)
    y = y_ref[...] + carried + skip_ref[...] * x_ref[0].astype(f32)
    z = z_ref[0].astype(f32)
    gated = y * (z / (1.0 + jnp.exp(-z)))
    scale = lax.rsqrt(jnp.mean(gated * gated, axis=1, keepdims=True) + norm_eps)
    o_ref[0] = (gated * scale * gain_ref[...]).astype(bf16)


def project_kernel(order_ref, a_ref, *refs):
    weights, o_ref = refs[:-1], refs[-1]
    depth = weights[0].shape[1]
    total = jnp.zeros(o_ref.shape[1:], f32)
    for i, w_ref in enumerate(weights):
        start = pl.multiple_of(order_ref[i] * depth, depth)
        total = total + jnp.dot(
            a_ref[:, pl.ds(start, depth)], w_ref[0], preferred_element_type=f32
        )
    o_ref[0] = total.astype(bf16)


def params(**more):
    return pltpu.CompilerParams(vmem_limit_bytes=VMEM_LIMIT, **more)


def shards(
    head_input,
    gate_input,
    state_in_proj,
    state_out_proj,
    step_raw,
    head_step_bias,
    decay_log,
    skip_gain,
    norm_gain,
    out_weight,
    pool_states,
    slot_map,
    span_lengths,
):
    ctx_count = lax.axis_size("ctx")
    ctx_index = lax.axis_index("ctx")
    sess_index = lax.axis_index("sess")
    head_index = lax.axis_index("head")
    group_index = lax.axis_index("groups")
    group_axis = lax.axis_size("groups")
    sess_axis = lax.axis_size("sess")
    sessions, tokens, inner = head_input.shape
    heads = step_raw.shape[2]
    head_dim = inner // heads
    state_cols = pool_states.shape[3]
    state_size = state_in_proj.shape[3]
    group_heads = HEADS // GROUPS
    count = heads // group_heads
    channels = group_heads * head_dim
    first_session = sess_index * sessions

    replicas = group_axis * sess_axis
    depth = out_weight.shape[0] // replicas
    own_cols = out_weight.shape[1]
    unit = own_cols // 8
    first_row = (group_index * sess_axis + sess_index) * depth

    def gathered(k, after=None):
        offset = sum(CHUNK_EIGHTHS[:k]) * unit
        width = CHUNK_EIGHTHS[k] * unit
        block = lax.dynamic_slice(out_weight, (first_row, offset), (depth, width))
        if after is not None:
            block, after = lax.optimization_barrier((block, after))
        mine = lax.all_gather(block, "ctx", axis=0)
        across = swapped(mine, "groups")
        return (mine, swapped(mine, "sess"), across, swapped(across, "sess")), after

    weights = [gathered(k)[0] for k in range(2)]
    other_group = group_axis - 1 - group_index
    other_sess = sess_axis - 1 - sess_index
    order = jnp.stack(
        [
            group_index * sess_axis + sess_index,
            group_index * sess_axis + other_sess,
            other_group * sess_axis + sess_index,
            other_group * sess_axis + other_sess,
        ]
    ).astype(jnp.int32)

    own_pool = jnp.transpose(pool_states, (0, 1, 3, 2))
    other_pool = swapped(own_pool.astype(bf16), "sess")
    own_slots = lax.dynamic_slice_in_dim(slot_map, first_session, sessions)
    slots = jnp.stack([own_slots % own_pool.shape[0], own_slots // own_pool.shape[0] - sess_index])

    own_lengths = lax.dynamic_slice_in_dim(span_lengths, first_session, sessions)
    position = ctx_index * tokens + jnp.arange(tokens, dtype=jnp.int32)
    live_rows = (position[None, :] < own_lengths[:, None] * SPAN).astype(f32)
    size = jax.nn.softplus(step_raw + head_step_bias) * live_rows[:, :, None]
    log_keep = -jnp.exp(decay_log) * size
    lower = jnp.tril(jnp.ones((tokens, tokens), f32))
    cum = jnp.einsum("lm,smh->slh", lower, log_keep, precision=lax.Precision.HIGHEST)
    shard_log = cum[:, -1, :]
    tail = jnp.exp(cum[:, -1:, :] - cum) * size

    def by_group(value):
        return jnp.moveaxis(value.reshape(sessions, tokens, count, group_heads), 2, 1)

    def by_group_t(value):
        return jnp.transpose(value, (0, 2, 1)).reshape(sessions, count, group_heads, tokens)

    first_group = head_index * heads // group_heads
    b_groups = jnp.moveaxis(lax.dynamic_slice_in_dim(state_in_proj, first_group, count, 2), 2, 1)
    c_groups = jnp.moveaxis(lax.dynamic_slice_in_dim(state_out_proj, first_group, count, 2), 2, 1)

    wide = pl.BlockSpec((1, tokens, channels), lambda s, g: (s, 0, g))
    square = pl.BlockSpec((1, 1, tokens, state_size), lambda s, g: (s, g, 0, 0))
    tall = pl.BlockSpec((1, 1, tokens, group_heads), lambda s, g: (s, g, 0, 0))
    flat = pl.BlockSpec((1, 1, group_heads, tokens), lambda s, g: (s, g, 0, 0))
    states = pl.BlockSpec((ctx_count, 1, state_cols, channels), lambda s, g: (0, s, 0, g))
    line = pl.BlockSpec((1, channels), lambda s, g: (0, g))
    work = sessions * count * tokens

    local_end = pl.pallas_call(
        functools.partial(local_end_kernel, head_dim),
        grid=(sessions, count),
        in_specs=[wide, square, tall],
        out_specs=states,
        out_shape=jax.ShapeDtypeStruct((ctx_count, sessions, state_cols, inner), bf16),
        compiler_params=params(),
        cost_estimate=pl.CostEstimate(
            flops=2 * work * state_size * channels,
            bytes_accessed=4 * work * channels,
            transcendentals=0,
        ),
    )(head_input, b_groups, by_group(tail))

    ends = lax.all_to_all(local_end, "ctx", 0, 0)
    logs = lax.all_to_all(
        jnp.broadcast_to(shard_log, (ctx_count,) + shard_log.shape), "ctx", 0, 0
    )
    logs = jnp.transpose(logs.reshape(ctx_count, sessions, count, group_heads), (1, 2, 0, 3))
    pool_block = pl.BlockSpec(
        (1, group_heads, state_cols, head_dim), lambda s, g, slots: (slots[0, s], g, 0, 0)
    )
    states_p = pl.BlockSpec(
        (ctx_count, 1, state_cols, channels), lambda s, g, slots: (0, s, 0, g)
    )
    entering, final = pl.pallas_call(
        functools.partial(combine_kernel, head_dim),
        grid_spec=pltpu.PrefetchScalarGridSpec(
            num_scalar_prefetch=1,
            grid=(sessions, count),
            in_specs=[
                states_p,
                pl.BlockSpec((1, 1, ctx_count, group_heads), lambda s, g, slots: (s, g, 0, 0)),
                pool_block,
                pool_block,
            ],
            out_specs=[
                states_p,
                pl.BlockSpec(
                    (1, group_heads, state_cols, head_dim), lambda s, g, slots: (s, g, 0, 0)
                ),
            ],
        ),
        out_shape=[
            jax.ShapeDtypeStruct((ctx_count, sessions, state_cols, inner), bf16),
            jax.ShapeDtypeStruct((sessions, heads, state_cols, head_dim), f32),
        ],
        compiler_params=params(),
        cost_estimate=pl.CostEstimate(
            flops=3 * ctx_count * sessions * state_cols * inner,
            bytes_accessed=6 * ctx_count * sessions * state_cols * inner,
            transcendentals=0,
        ),
    )(slots, ends, logs, own_pool, other_pool)
    final_states = jnp.transpose(final, (0, 1, 3, 2))
    chunk, entering = gathered(2, entering)
    weights.append(chunk)
    chunk, entering = gathered(3, entering)
    weights.append(chunk)
    carried = lax.all_to_all(entering, "ctx", 0, 0)
    carried, crossed = lax.optimization_barrier((carried, weights[1][2]))
    weights[1] = weights[1][:2] + (crossed, swapped(crossed, "sess"))

    normed = pl.pallas_call(
        functools.partial(normed_kernel, head_dim),
        grid=(sessions, count),
        in_specs=[wide, wide, square, square, tall, flat, flat, states, line, line],
        out_specs=wide,
        out_shape=jax.ShapeDtypeStruct((sessions, tokens, inner), bf16),
        scratch_shapes=[pltpu.VMEM((tokens, channels), f32)],
        compiler_params=params(),
        cost_estimate=pl.CostEstimate(
            flops=2 * work * channels * 3 * state_size,
            bytes_accessed=8 * work * channels,
            transcendentals=work * (channels + tokens * group_heads),
        ),
    )(
        head_input,
        gate_input,
        b_groups,
        c_groups,
        by_group(cum),
        by_group_t(cum),
        by_group_t(size),
        carried,
        jnp.repeat(skip_gain, head_dim)[None, :],
        norm_gain[None, :],
    ).reshape(sessions * tokens, inner)

    chunk, normed = gathered(4, normed)
    weights.append(chunk)

    rows = sessions * tokens
    own_shards = ctx_count // lax.axis_size("head")
    sums = []
    for chunk in weights:
        chunk_cols = chunk[0].shape[2]
        part = pl.pallas_call(
            project_kernel,
            grid_spec=pltpu.PrefetchScalarGridSpec(
                num_scalar_prefetch=1,
                grid=(ctx_count,),
                in_specs=[pl.BlockSpec((rows, inner), lambda c, order: (0, 0))]
                + [pl.BlockSpec((1, depth, chunk_cols), lambda c, order: (c, 0, 0))] * replicas,
                out_specs=pl.BlockSpec((1, rows, chunk_cols), lambda c, order: (c, 0, 0)),
            ),
            out_shape=jax.ShapeDtypeStruct((ctx_count, rows, chunk_cols), bf16),
            compiler_params=params(),
            cost_estimate=pl.CostEstimate(
                flops=2 * rows * inner * ctx_count * chunk_cols,
                bytes_accessed=2 * inner * (rows + ctx_count * chunk_cols),
                transcendentals=0,
            ),
        )(order, normed, *chunk)
        if own_shards * 2 == ctx_count:
            kept = lax.dynamic_slice_in_dim(part, head_index * own_shards, own_shards)
            sent = lax.dynamic_slice_in_dim(part, (1 - head_index) * own_shards, own_shards)
            total = kept.astype(f32) + swapped(sent, "head").astype(f32)
        else:
            total = lax.psum_scatter(part, "head", scatter_dimension=0, tiled=True).astype(f32)
        total = total.reshape(own_shards, sessions, tokens, chunk_cols)
        sums.append((total * live_rows[None, :, :, None]).astype(bf16))
    mixed = jnp.concatenate(
        [total[shard] for shard in range(own_shards) for total in sums], axis=2
    )
    return (mixed, final_states)


def solution(mesh):
    placed = (
        P(("groups", "sess"), "ctx", "head"),
        P(("groups", "sess"), "ctx", "head"),
        P(("groups", "sess"), "ctx", None, None),
        P(("groups", "sess"), "ctx", None, None),
        P(("groups", "sess"), "ctx", "head"),
        P("head"),
        P("head"),
        P("head"),
        P("head"),
        P("head", "ctx"),
        P(("groups", "sess"), "head", None, "ctx"),
        P("groups"),
        P("groups"),
    )
    return jax.shard_map(
        shards,
        mesh=mesh,
        in_specs=placed,
        out_specs=(
            P(("groups", "sess"), "ctx", "head"),
            P(("groups", "sess"), "head", None, "ctx"),
        ),
        check_vma=False,
    )
```
